256 devices in a mesh: seq: 128 (over y, z, x), batch: 2 (over core).
Axes of the slice: x: 4, y: 4, z: 8, core: 2. Of those that a mesh axis runs over, the one named last changes fastest.
Arguments:
- points: bfloat16 [2, 131072, 256], P('batch', 'seq'), may hold values from -6 to 6
- gain: float32 [256], replicated, may hold values from 0.5 to 1.5
- w_qkv: bfloat16 [256, 768], replicated
- w_out: bfloat16 [256, 256], replicated, may hold values from -0.375 to 0.375
- route: int32 [2, 1024], P('batch', 'seq'), may hold values from 0 to 1023, as said below
- order: int32 [2, 128, 1024], P('batch', 'seq'), may hold values from 0 to 1023, each once within a row
- pattern: int32 [2, 256, 4, 4], P('batch', 'seq'), may hold values 0 or 1
- grad_out: bfloat16 [2, 131072, 256], P('batch', 'seq'), may hold values from -6 to 6
Outputs:
- result: bfloat16 [2, 131072, 256], P('batch', 'seq')
- grad_points: bfloat16 [2, 131072, 256], P('batch', 'seq')
- grad_gain: float32 [256], replicated
- grad_w_qkv: float32 [256, 768], replicated
- grad_w_out: float32 [256, 256], replicated
The draws below stay inside these ranges and needn't reach their ends.
Inputs may be any that keep to these rules, and one draw needn't show every extreme that they name: For each sample, route is a permutation of the 1024 slot numbers. Slot s goes to a device (route // 8) within 2 of its own device s // 8; one device sends at most 2 slots to any one other device and receives as many back from it; in every sample some pair of devices exchanges exactly 2.
All inputs are finite; a program needn't handle non-finite values. No bound on the sum of `pattern` on one device may be relied on, other than what follows from the above.
Results may differ from the reference program's by a relative error of at most 0.0085.
The reference program's roundings to bfloat16 on the way count: a program that leaves them out, or rounds other values in their place, can miss the bound.
Values may be sent and summed in bfloat16 or wider, within the bound.
No kernel may reach another device: no remote copies, remote signals or barrier semaphores. Data moves between devices by JAX's collectives and lax.ppermute only.
A program may use at most 128 MiB of HBM per device.

```python
import jax
import jax.numpy as jnp
from jax import lax

D = 256
HEADS = 8
WINDOW = 512
SLOT = 128
HOP = 2
MOST = 2
ROWS = 1024
SLOT_DEV = 8
BLK = 4
POINTS = 131072
SLOTS = 1024
WINDOWS = 256
BATCH = 2
N_SEQ = 128


def draw_w_qkv(key, part):
    first = jax.random.fold_in(key, 0)
    base = jax.random.normal(first, (D, 3 * D), jnp.float32) * D ** (-0.5)
    return base.astype(jnp.bfloat16)


def block_of(relative):
    return jnp.where(relative < 0, relative + HOP, relative + HOP - 1)


def draw_route(key, part):
    devices = SLOTS // SLOT_DEV

    def one_sample(sample_key):
        first, second, third, fourth = jax.random.split(sample_key, 4)
        amounts = jax.random.randint(first, (devices, HOP), 0, MOST + 1)
        device_ids = jnp.arange(devices, dtype=jnp.int32)[:, None]
        distances = jnp.arange(1, HOP + 1, dtype=jnp.int32)[None, :]
        amounts = jnp.where(device_ids + distances < devices, amounts, 0)
        forced_device = jax.random.randint(second, (), 0, devices - HOP)
        forced_distance = jax.random.randint(third, (), 0, HOP)
        amounts = amounts.at[forced_device, forced_distance].set(MOST)
        shuffles = jax.vmap(lambda sub_key: jax.random.permutation(sub_key, SLOT_DEV))(jax.random.split(fourth, devices)).astype(jnp.int32)
        source_dev = jnp.broadcast_to(device_ids[:, :, None], (devices, HOP, MOST))
        distance = jnp.broadcast_to(distances[:, :, None], (devices, HOP, MOST))
        member = jnp.broadcast_to(jnp.arange(MOST, dtype=jnp.int32)[None, None, :], (devices, HOP, MOST))
        active = member < amounts[:, :, None]
        partner = jnp.minimum(source_dev + distance, devices - 1)
        source_spot = shuffles[source_dev, block_of(distance) * MOST + member]
        partner_spot = shuffles[partner, block_of(-distance) * MOST + member]
        source_slot = source_dev * SLOT_DEV + source_spot
        partner_slot = partner * SLOT_DEV + partner_spot
        identity = jnp.arange(SLOTS, dtype=jnp.int32)
        outside = jnp.full(source_slot.shape, SLOTS, jnp.int32)
        where_from = jnp.concatenate([jnp.where(active, source_slot, outside).reshape(-1), jnp.where(active, partner_slot, outside).reshape(-1)])
        where_to = jnp.concatenate([partner_slot.reshape(-1), source_slot.reshape(-1)])
        return identity.at[where_from].set(where_to, mode='drop')
    return jax.vmap(one_sample)(jax.random.split(key, BATCH))


def touch_ends(entries, own_key, smallest, top_value):
    longest = entries.shape.index(max(entries.shape))
    spots = []
    for shift in (0, 1):
        where = [jax.random.randint(jax.random.fold_in(own_key, axis), (), 0, length) for axis, length in enumerate(entries.shape)]
        where[longest] = (where[longest] + shift) % entries.shape[longest]
        spots.append(tuple(where))
    return entries.at[spots[0]].set(smallest).at[spots[1]].set(top_value)


def shard_levels(key, dims, cuts, least, high):
    loudness = 1.0
    for axis_at, shards_of in cuts:
        steps = jax.random.uniform(jax.random.fold_in(jax.random.fold_in(key, 6), axis_at), (shards_of,), jnp.float32, least / len(cuts), high / len(cuts))
        loudness = loudness * jnp.repeat(jnp.exp(steps), dims[axis_at] // shards_of).reshape((-1,) + (1,) * (len(dims) - 1 - axis_at))
    return loudness


def scatter_about(key, shape, spread, reach, cuts=(), held_as=jnp.bfloat16):
    entries = spread * jax.random.normal(key, shape, jnp.float32)
    if cuts:
        entries = entries * shard_levels(key, shape, cuts, -0.22, 0.18)
    return jnp.clip(entries, -reach, reach).astype(held_as)


def setup_inputs(seed: int = 0) -> dict:
    arg_keys = jax.random.split(jax.random.key(seed), 9)
    points = scatter_about(arg_keys[0], (BATCH, POINTS, D), 1.0, 6.0, ((0, 2), (1, 128)))
    gain = jnp.clip(1.0 + 0.1 * jax.random.normal(arg_keys[1], (D,), jnp.float32), 0.5, 1.5)
    w_qkv = draw_w_qkv(jax.random.fold_in(arg_keys[8], 71), 0)
    w_out = scatter_about(arg_keys[3], (D, D), D ** -0.5, 0.375)
    route = draw_route(jax.random.fold_in(arg_keys[8], 71), 0)
    order = jax.vmap(lambda own: jax.random.permutation(own, ROWS))(jax.random.split(arg_keys[5], BATCH * N_SEQ)).reshape((BATCH, N_SEQ, ROWS)).astype(jnp.int32)
    pattern = touch_ends((jax.random.randint(arg_keys[6], (BATCH, WINDOWS, BLK, BLK), 0, 4) < 3).astype(jnp.int32), jax.random.fold_in(arg_keys[6], 1), 0, 1)
    grad_out = scatter_about(arg_keys[7], (BATCH, POINTS, D), 1.0, 6.0, ((0, 2), (1, 128)))
    return {"points": points, "gain": gain, "w_qkv": w_qkv, "w_out": w_out, "route": route, "order": order, "pattern": pattern, "grad_out": grad_out}


EPSILON = 1e-05

def multiply(form, left, right):
    return jnp.einsum(form, left.astype(jnp.float32), right.astype(jnp.float32))

def norm_stats(window_rows):
    as_float = window_rows.astype(jnp.float32)
    centred = as_float - lax.optimization_barrier(jnp.mean(as_float, axis=-1, keepdims=True))
    inverse_std = lax.rsqrt(lax.optimization_barrier(jnp.mean(centred * centred, axis=-1, keepdims=True)) + EPSILON)
    return (as_float, centred * inverse_std, inverse_std)

def block_probs(qkv, allowed, start, amount, heads, slot):
    total_rows = qkv.shape[0]
    width = qkv.shape[1] // 3
    head_dim = width // heads
    queries = qkv[start:start + amount, :width].reshape(amount, heads, head_dim)
    keys_all = qkv[:, width:2 * width].reshape(total_rows, heads, head_dim)
    scores = multiply('qhd,khd->hqk', queries, keys_all) * head_dim ** (-0.5)
    block_rows = jnp.repeat(allowed, slot, axis=0)[start:start + amount]
    visible = jnp.repeat(block_rows, slot, axis=1)
    scores = jnp.where(visible[None], scores, -jnp.inf)
    highest = lax.optimization_barrier(jnp.max(scores, axis=-1, keepdims=True))
    powers = jnp.exp(scores - highest)
    return powers / lax.optimization_barrier(jnp.sum(powers, axis=-1, keepdims=True))

def window_forward(window_rows, gain, w_qkv, w_out, allowed, heads, slot):
    as_float, normalized, inverse_std = norm_stats(window_rows)
    normed = (normalized * gain).astype(jnp.bfloat16)
    qkv = jnp.dot(normed, w_qkv, preferred_element_type=jnp.float32).astype(jnp.bfloat16)
    total_rows, width = window_rows.shape
    head_dim = width // heads
    values_all = qkv[:, 2 * width:].reshape(total_rows, heads, head_dim)
    query_step = min(512, total_rows)
    pieces = []
    for start in range(0, total_rows, query_step):
        rounded = block_probs(qkv, allowed, start, query_step, heads, slot).astype(jnp.bfloat16)
        blended = multiply('hqk,khd->qhd', rounded, values_all)
        pieces.append(blended.reshape(query_step, width).astype(jnp.bfloat16))
    mixed = jnp.concatenate(pieces, axis=0)
    output = (as_float + jnp.dot(mixed, w_out, preferred_element_type=jnp.float32)).astype(jnp.bfloat16)
    return (output, (normed, qkv, mixed, normalized, inverse_std))

def window_backward(grad_rows, gain, w_qkv, w_out, allowed, saved, heads, slot):
    normed, qkv, mixed, normalized, inverse_std = saved
    total_rows, width = grad_rows.shape
    head_dim = width // heads
    d_mixed = jnp.dot(grad_rows, w_out.T, preferred_element_type=jnp.float32).astype(jnp.bfloat16)
    g_out = jnp.dot(mixed.T, grad_rows, preferred_element_type=jnp.float32)
    queries = qkv[:, :width].reshape(total_rows, heads, head_dim)
    keys_all = qkv[:, width:2 * width].reshape(total_rows, heads, head_dim)
    values_all = qkv[:, 2 * width:].reshape(total_rows, heads, head_dim)
    d_keys = jnp.zeros((total_rows, heads, head_dim), jnp.float32)
    d_values = jnp.zeros((total_rows, heads, head_dim), jnp.float32)
    query_step = min(512, total_rows)
    d_query_parts = []
    for start in range(0, total_rows, query_step):
        probs = block_probs(qkv, allowed, start, query_step, heads, slot)
        rounded = probs.astype(jnp.bfloat16)
        d_block = d_mixed[start:start + query_step].reshape(query_step, heads, head_dim)
        d_values = d_values + multiply('hqk,qhd->khd', rounded, d_block)
        d_probs = multiply('qhd,khd->hqk', d_block, values_all)
        d_scores = probs * (d_probs - lax.optimization_barrier(jnp.sum(d_probs * probs, axis=-1, keepdims=True))) * head_dim ** (-0.5)
        d_scores = d_scores.astype(jnp.bfloat16)
        d_query_parts.append(multiply('hqk,khd->qhd', d_scores, keys_all).reshape(query_step, width))
        d_keys = d_keys + multiply('hqk,qhd->khd', d_scores, queries[start:start + query_step])
    d_qkv = jnp.concatenate([jnp.concatenate(d_query_parts, axis=0), d_keys.reshape(total_rows, width), d_values.reshape(total_rows, width)], axis=1).astype(jnp.bfloat16)
    g_qkv = jnp.dot(normed.T, d_qkv, preferred_element_type=jnp.float32)
    d_normed = jnp.dot(d_qkv, w_qkv.T, preferred_element_type=jnp.float32)
    g_gain = lax.optimization_barrier(jnp.sum(d_normed * normalized, axis=0))
    d_hat = d_normed * gain
    branch = inverse_std * (d_hat - lax.optimization_barrier(jnp.mean(d_hat, axis=-1, keepdims=True)) - normalized * lax.optimization_barrier(jnp.mean(d_hat * normalized, axis=-1, keepdims=True)))
    d_rows = (grad_rows.astype(jnp.float32) + branch).astype(jnp.bfloat16)
    return (d_rows, g_gain, g_qkv, g_out)

def take_rows(block_rows, positions):
    return block_rows[positions]

def put_rows(block_rows, positions):
    return jnp.zeros_like(block_rows).at[positions].set(block_rows)

def to_hilbert(features, sample_route, sample_order):
    width = features.shape[1]
    slots = features.reshape(SLOTS, SLOT, width)
    arrived = jnp.zeros_like(slots).at[sample_route].set(slots).reshape(N_SEQ, ROWS, width)
    placed = jax.vmap(take_rows)(arrived, sample_order)
    return placed.reshape(WINDOWS, WINDOW, width)

def to_zorder(features, sample_route, sample_order):
    width = features.shape[2]
    arrived = features.reshape(N_SEQ, ROWS, width)
    restored = jax.vmap(put_rows)(arrived, sample_order).reshape(SLOTS, SLOT, width)
    return restored[sample_route].reshape(POINTS, width)

def reference(points, gain, w_qkv, w_out, route, order, pattern, grad_out):
    width = points.shape[2]
    totals = (jnp.zeros((width,), jnp.float32), jnp.zeros((width, 3 * width), jnp.float32), jnp.zeros((width, width), jnp.float32))
    outputs = []
    gradients = []
    for sample in range(BATCH):
        hilbert = to_hilbert(points[sample], route[sample], order[sample])
        upstream = to_hilbert(grad_out[sample], route[sample], order[sample])
        allowed = (pattern[sample] > 0) | jnp.eye(BLK, dtype=bool)[None]

        def visit(carry, inputs):
            window_rows, window_grad, window_allowed = inputs
            output, saved = window_forward(window_rows, gain, w_qkv, w_out, window_allowed, HEADS, SLOT)
            d_rows, g_gain, g_qkv, g_out = window_backward(window_grad, gain, w_qkv, w_out, window_allowed, saved, HEADS, SLOT)
            return ((carry[0] + g_gain, carry[1] + g_qkv, carry[2] + g_out), (output, d_rows))
        totals, (window_out, window_dx) = lax.scan(visit, totals, (hilbert, upstream, allowed))
        outputs.append(to_zorder(window_out, route[sample], order[sample]))
        gradients.append(to_zorder(window_dx, route[sample], order[sample]))
    factor = (BATCH * POINTS) ** (-0.5)
    return (jnp.stack(outputs), jnp.stack(gradients), totals[0] * factor, totals[1] * factor, totals[2] * factor)
```

```python
import functools

import jax
import jax.numpy as jnp
from jax import lax
from jax.experimental import pallas as pl
from jax.experimental.pallas import tpu as pltpu
from jax.sharding import PartitionSpec as P

HEADS = 8
WINDOW = 512
SLOT = 128
BLK = WINDOW // SLOT
DISTANCES = (-2, -1, 1, 2)
MOST = 2
LABEL_ROWS = 16
EPSILON = 1e-05
LOG2E = 1.4426950408889634

BF16 = jnp.bfloat16
F32 = jnp.float32


def dot(left, right):
    return lax.dot_general(left, right, (((1,), (0,)), ((), ())), preferred_element_type=F32)


def dot_nt(left, right):
    return lax.dot_general(left, right, (((1,), (1,)), ((), ())), preferred_element_type=F32)


def dot_tn(left, right):
    return lax.dot_general(left, right, (((0,), (0,)), ((), ())), preferred_element_type=F32)


def slot_moves(rel_ref, amount):
    moves = []
    for s in range(amount):
        value = rel_ref[s] + 8 * amount
        moves.append((value // amount - 8, lax.rem(value, amount)))
    return moves


def pack_kernel(rel_ref, points_ref, grads_ref, *outs):
    amount = points_ref.shape[0] // SLOT
    width = points_ref.shape[1]
    moves = slot_moves(rel_ref, amount)
    point_outs, grad_outs = outs[:4], outs[4:]
    lane = lax.broadcasted_iota(jnp.int32, (LABEL_ROWS, width), 1)
    for out in outs:
        out[...] = jnp.zeros_like(out)
    for point_out, grad_out, distance in zip(point_outs, grad_outs, DISTANCES):
        count = jnp.int32(0)
        first = jnp.int32(0)
        second = jnp.int32(0)
        for s, (offset, spot) in enumerate(moves):
            goes = offset == distance

            @pl.when(goes)
            def _(s=s, count=count):
                start = pl.multiple_of(jnp.minimum(count, MOST - 1) * SLOT, SLOT)
                point_out[pl.ds(start, SLOT), :] = points_ref[s * SLOT : (s + 1) * SLOT, :]
                grad_out[pl.ds(start, SLOT), :] = grads_ref[s * SLOT : (s + 1) * SLOT, :]

            first = jnp.where(goes & (count == 0), spot + 1, first)
            second = jnp.where(goes & (count == 1), spot + 1, second)
            count = count + goes.astype(jnp.int32)
        labels = jnp.where(lane < SLOT, first, second).astype(F32).astype(BF16)
        point_out[MOST * SLOT :, :] = labels


def restore_kernel(rel_ref, local_ref, *refs):
    arrivals, out_ref = refs[:4], refs[4]
    amount = local_ref.shape[0] // SLOT
    moves = slot_moves(rel_ref, amount)
    counts = [jnp.int32(0)] * 4
    for s, (offset, _) in enumerate(moves):
        rows = slice(s * SLOT, (s + 1) * SLOT)

        @pl.when(offset == 0)
        def _(rows=rows):
            out_ref[rows, :] = local_ref[rows, :]

        for number, distance in enumerate(DISTANCES):
            goes = offset == distance

            @pl.when(goes)
            def _(rows=rows, number=number, count=counts[number]):
                start = pl.multiple_of(jnp.minimum(count, MOST - 1) * SLOT, SLOT)
                out_ref[rows, :] = arrivals[number][pl.ds(start, SLOT), :]

            counts[number] = counts[number] + goes.astype(jnp.int32)


def landing_rows(rel_ref, label_refs, amount):
    rows = []
    for offset, spot in slot_moves(rel_ref, amount):
        landing = jnp.where(offset == 0, spot, -1) * SLOT
        rows.append(jnp.full((1, SLOT), landing, jnp.int32))
    for label in label_refs:
        held = label[0:1, :].astype(F32).astype(jnp.int32)
        for number in range(MOST):
            rows.append((held[:, number * SLOT : (number + 1) * SLOT] - 1) * SLOT)
    return rows


def build_gather(order_ref, rows, place_ref):
    total = order_ref.shape[1]
    order = jnp.broadcast_to(order_ref[...].astype(F32), (SLOT, total))
    column = jnp.transpose(order).astype(jnp.int32)
    lane = lax.broadcasted_iota(jnp.int32, (1, SLOT), 1)
    for number, row in enumerate(rows):
        place_ref[:, number * SLOT : (number + 1) * SLOT] = (
            jnp.where(column == row + lane, 1.0, 0.0).astype(BF16)
        )


def build_scatter(order_ref, rows, spread_ref):
    total = order_ref.shape[1]
    inside = lax.broadcasted_iota(jnp.int32, (SLOT, total), 0)
    for number, row in enumerate(rows):
        wide = jnp.concatenate([row] * (total // SLOT), axis=1)
        spread_ref[number * SLOT : (number + 1) * SLOT, :] = (
            jnp.where(order_ref[...] - wide == inside, 1.0, 0.0).astype(BF16)
        )


def bias_rows(pattern_ref, window):
    rows = []
    for key_block in range(BLK):
        pieces = []
        for query_block in range(BLK):
            if query_block == key_block:
                pieces.append(jnp.zeros((1, SLOT), F32))
            else:
                seen = pattern_ref[window * BLK * BLK + query_block * BLK + key_block] > 0
                pieces.append(jnp.full((1, SLOT), jnp.where(seen, 0.0, -jnp.inf), F32))
        rows.append(jnp.concatenate(pieces, axis=1))
    return rows


def by_block(rows):
    return jnp.concatenate([row[None] for row in rows], axis=0)


def norm_stats(rows):
    as_float = rows.astype(F32)
    centred = as_float - jnp.mean(as_float, axis=-1, keepdims=True)
    inverse_std = lax.rsqrt(jnp.mean(centred * centred, axis=-1, keepdims=True) + EPSILON)
    return as_float, centred * inverse_std, inverse_std


def forward_kernel(
    rel_ref,
    pattern_ref,
    order_ref,
    points_ref,
    a0,
    a1,
    a2,
    a3,
    gain_ref,
    w_qkv_ref,
    w_qkv_t_ref,
    w_out_ref,
    local_ref,
    r0,
    r1,
    r2,
    r3,
    hilbert_ref,
    qkv_ref,
    qk_t_ref,
    mixed_t_ref,
    lse_ref,
    place_ref,
    spread_ref,
    source_ref,
    v_t_ref,
    out_ref,
):
    arrivals = (a0, a1, a2, a3)
    returns = (r0, r1, r2, r3)
    total, width = points_ref.shape
    head_dim = width // HEADS
    factor = head_dim ** (-0.5) * LOG2E
    source_ref[0:total, :] = points_ref[...]
    for number, arrival in enumerate(arrivals):
        start = total + number * MOST * SLOT
        source_ref[start : start + MOST * SLOT, :] = arrival[0 : MOST * SLOT, :]
    labels = [arrival.at[MOST * SLOT : MOST * SLOT + LABEL_ROWS] for arrival in arrivals]
    rows = landing_rows(rel_ref, labels, total // SLOT)
    build_gather(order_ref, rows, place_ref)
    hilbert_ref[...] = dot(place_ref[...], source_ref[...]).astype(BF16)
    build_scatter(order_ref, rows, spread_ref)

    @pl.loop(0, total // WINDOW)
    def _(window):
        span = pl.ds(pl.multiple_of(window * WINDOW, WINDOW), WINDOW)
        h = hilbert_ref[span, :]
        as_float, normalized, _ = norm_stats(h)
        normed = (normalized * gain_ref[...]).astype(BF16)
        qkv = dot(normed, w_qkv_ref[...]).astype(BF16)
        qkv_ref[span, :] = qkv
        qkv_t = dot_nt(w_qkv_t_ref[...], normed).astype(BF16)
        qk_t_ref[window] = qkv_t[: 2 * width]
        v_t_ref[...] = qkv_t[2 * width :]
        bias = by_block(bias_rows(pattern_ref, window))
        for head in range(HEADS):
            low = head * head_dim
            keys = qkv_ref[span, width + low : width + low + head_dim]
            queries_t = qk_t_ref[window, low : low + head_dim, :]
            scores = dot(keys, queries_t).reshape(BLK, SLOT, WINDOW) + bias
            highest = jnp.max(scores, axis=(0, 1), keepdims=True)
            powers = jnp.exp2((scores - highest) * factor)
            total_power = jnp.sum(powers, axis=(0, 1), keepdims=True)
            probs = (powers * (1.0 / total_power)).astype(BF16).reshape(WINDOW, WINDOW)
            mixed_t = dot(v_t_ref[low : low + head_dim, :], probs)
            mixed_t_ref[window, low : low + head_dim, :] = mixed_t.astype(BF16)
            lse = highest * factor + jnp.log2(total_power)
            lse_ref[window, head : head + 1, :] = lse.reshape(1, WINDOW)
        mixed = jnp.transpose(mixed_t_ref[window])
        out_ref[span, :] = (as_float + dot(mixed, w_out_ref[...])).astype(BF16)

    out = out_ref[...]
    local_ref[...] = dot(spread_ref[0:total, :], out).astype(BF16)
    for number, back in enumerate(returns):
        start = total + number * MOST * SLOT
        back[...] = dot(spread_ref[start : start + MOST * SLOT, :], out).astype(BF16)


def backward_kernel(
    rel_ref,
    pattern_ref,
    order_ref,
    grads_ref,
    a0,
    a1,
    a2,
    a3,
    l0,
    l1,
    l2,
    l3,
    gain_ref,
    w_qkv_ref,
    w_out_ref,
    hilbert_ref,
    qkv_ref,
    qk_t_ref,
    mixed_t_ref,
    lse_ref,
    local_ref,
    r0,
    r1,
    r2,
    r3,
    sums_ref,
    place_ref,
    spread_ref,
    source_ref,
    upstream_ref,
    d_rows_ref,
    d_kv_ref,
    d_q_t_ref,
    d_mixed_t_ref,
    g_qkv_ref,
    g_out_ref,
    g_gain_ref,
):
    arrivals = (a0, a1, a2, a3)
    returns = (r0, r1, r2, r3)
    total, width = grads_ref.shape
    head_dim = width // HEADS
    scale = head_dim ** (-0.5)
    factor = scale * LOG2E
    source_ref[0:total, :] = grads_ref[...]
    for number, arrival in enumerate(arrivals):
        start = total + number * MOST * SLOT
        source_ref[start : start + MOST * SLOT, :] = arrival[...]
    rows = landing_rows(rel_ref, (l0, l1, l2, l3), total // SLOT)
    build_gather(order_ref, rows, place_ref)
    upstream_ref[...] = dot(place_ref[...], source_ref[...]).astype(BF16)
    build_scatter(order_ref, rows, spread_ref)
    g_qkv_ref[...] = jnp.zeros_like(g_qkv_ref)
    g_out_ref[...] = jnp.zeros_like(g_out_ref)
    g_gain_ref[...] = jnp.zeros_like(g_gain_ref)

    @pl.loop(0, total // WINDOW)
    def _(window):
        span = pl.ds(pl.multiple_of(window * WINDOW, WINDOW), WINDOW)
        upstream = upstream_ref[span, :]
        g_out_ref[...] += dot(mixed_t_ref[window], upstream)
        d_mixed = dot_nt(upstream, w_out_ref[...]).astype(BF16)
        d_mixed_t_ref[...] = dot_nt(w_out_ref[...], upstream).astype(BF16)
        bias = by_block(bias_rows(pattern_ref, window))
        for head in range(HEADS):
            low = head * head_dim
            high = low + head_dim
            queries = qkv_ref[span, low:high]
            keys = qkv_ref[span, width + low : width + high]
            values = qkv_ref[span, 2 * width + low : 2 * width + high]
            queries_t = qk_t_ref[window, low:high, :]
            keys_t = qk_t_ref[window, width + low : width + high, :]
            shift = bias - lse_ref[window, head : head + 1, :].reshape(1, 1, WINDOW)
            scores = dot(keys, queries_t).reshape(BLK, SLOT, WINDOW)
            probs = jnp.exp2(scores * factor + shift).reshape(WINDOW, WINDOW)
            d_block = d_mixed[:, low:high]
            d_values = dot(probs.astype(BF16), d_block)
            d_probs = dot(values, d_mixed_t_ref[low:high, :])
            inner = jnp.sum(d_probs * probs, axis=0, keepdims=True)
            d_scores = (probs * (d_probs - inner) * scale).astype(BF16)
            d_keys = dot(d_scores, queries)
            d_q_t_ref[low:high, :] = dot(keys_t, d_scores)
            d_kv_ref[:, low:high] = d_keys
            d_kv_ref[:, width + low : width + high] = d_values
        d_q = jnp.transpose(d_q_t_ref[...])
        d_qkv = jnp.concatenate([d_q, d_kv_ref[...]], axis=1).astype(BF16)
        _, normalized, inverse_std = norm_stats(hilbert_ref[span, :])
        gain = gain_ref[...]
        normed = (normalized * gain).astype(BF16)
        g_qkv_ref[...] += dot_tn(normed, d_qkv)
        d_normed = dot_nt(d_qkv, w_qkv_ref[...])
        g_gain_ref[0:1, :] += jnp.sum(d_normed * normalized, axis=0, keepdims=True)
        d_hat = d_normed * gain
        branch = inverse_std * (
            d_hat
            - jnp.mean(d_hat, axis=-1, keepdims=True)
            - normalized * jnp.mean(d_hat * normalized, axis=-1, keepdims=True)
        )
        d_rows_ref[span, :] = (upstream.astype(F32) + branch).astype(BF16)

    d_rows = d_rows_ref[...]
    local_ref[...] = dot(spread_ref[0:total, :], d_rows).astype(BF16)
    for number, back in enumerate(returns):
        start = total + number * MOST * SLOT
        back[...] = dot(spread_ref[start : start + MOST * SLOT, :], d_rows).astype(BF16)
    half = width // 2
    sums_ref[...] = jnp.zeros_like(sums_ref)
    for number in range(3):
        block = g_qkv_ref[:, number * width : (number + 1) * width]
        sums_ref[2 * number, 0:half, :] = block[0:half]
        sums_ref[2 * number + 1, 0:half, :] = block[half:width]
    sums_ref[6, 0:half, :] = g_out_ref[0:half, :]
    sums_ref[7, 0:half, :] = g_out_ref[half:width, :]
    sums_ref[0, half : half + 8, :] = g_gain_ref[...]


def scale_kernel(factor, sums_ref, gain_ref, qkv_ref, out_ref):
    width = out_ref.shape[1]
    half = width // 2
    for number in range(3):
        cols = slice(number * width, (number + 1) * width)
        qkv_ref[0:half, cols] = sums_ref[2 * number, 0:half, :] * factor
        qkv_ref[half:width, cols] = sums_ref[2 * number + 1, 0:half, :] * factor
    out_ref[0:half, :] = sums_ref[6, 0:half, :] * factor
    out_ref[half:width, :] = sums_ref[7, 0:half, :] * factor
    gain_ref[...] = sums_ref[0, half : half + 1, :] * factor


VMEM = pl.BlockSpec(memory_space=pltpu.VMEM)
SMEM = pl.BlockSpec(memory_space=pltpu.SMEM)
PARAMS = pltpu.CompilerParams(vmem_limit_bytes=60000 * 1024)


def shape_of(*dims, dtype=BF16):
    return jax.ShapeDtypeStruct(dims, dtype)


def pack(rel, points, grads):
    width = points.shape[1]
    tall = MOST * SLOT + LABEL_ROWS
    outs = pl.pallas_call(
        pack_kernel,
        out_shape=[shape_of(tall, width)] * 4 + [shape_of(MOST * SLOT, width)] * 4,
        in_specs=[SMEM, VMEM, VMEM],
        out_specs=[VMEM] * 8,
        compiler_params=PARAMS,
        cost_estimate=pl.CostEstimate(flops=0, bytes_accessed=2 << 20, transcendentals=0),
        name="pack_slots",
    )(rel, points, grads)
    return outs[:4], outs[4:]


def restore(rel, local, arrivals):
    return pl.pallas_call(
        restore_kernel,
        out_shape=shape_of(*local.shape),
        in_specs=[SMEM] + [VMEM] * 5,
        out_specs=VMEM,
        compiler_params=PARAMS,
        cost_estimate=pl.CostEstimate(flops=0, bytes_accessed=3 << 19, transcendentals=0),
        name="restore_slots",
    )(rel, local, *arrivals)


def forward(rel, pattern, order, points, arrivals, gain, w_qkv, w_qkv_t, w_out):
    total, width = points.shape
    windows = total // WINDOW
    sources = total + 4 * MOST * SLOT
    outs = pl.pallas_call(
        forward_kernel,
        out_shape=[shape_of(total, width)]
        + [shape_of(MOST * SLOT, width)] * 4
        + [
            shape_of(total, width),
            shape_of(total, 3 * width),
            shape_of(windows, 2 * width, WINDOW),
            shape_of(windows, width, WINDOW),
            shape_of(windows, HEADS, WINDOW, dtype=F32),
        ],
        in_specs=[SMEM, SMEM] + [VMEM] * 10,
        out_specs=[VMEM] * 10,
        scratch_shapes=[
            pltpu.VMEM((total, sources), BF16),
            pltpu.VMEM((sources, total), BF16),
            pltpu.VMEM((sources, width), BF16),
            pltpu.VMEM((width, WINDOW), BF16),
            pltpu.VMEM((total, width), BF16),
        ],
        compiler_params=PARAMS,
        cost_estimate=pl.CostEstimate(
            flops=12 << 30, bytes_accessed=8 << 20, transcendentals=4 << 20
        ),
        name="window_forward",
    )(rel, pattern, order, points, *arrivals, gain, w_qkv, w_qkv_t, w_out)
    return outs[0], outs[1:5], outs[5:]


def backward(rel, pattern, order, grads, arrivals, labels, gain, w_qkv, w_out, saved):
    total, width = grads.shape
    sources = total + 4 * MOST * SLOT
    label_spec = pl.BlockSpec((LABEL_ROWS, width), lambda i: (MOST * SLOT // LABEL_ROWS, 0))
    whole = lambda array: pl.BlockSpec(array.shape, lambda i: (0,) * array.ndim)
    outs_shape = (
        [shape_of(total, width)]
        + [shape_of(MOST * SLOT, width)] * 4
        + [shape_of(8, width // 2 + 8, width, dtype=F32)]
    )
    outs = pl.pallas_call(
        backward_kernel,
        grid=(1,),
        out_shape=outs_shape,
        in_specs=[SMEM, SMEM]
        + [whole(array) for array in (order, grads, *arrivals)]
        + [label_spec] * 4
        + [whole(array) for array in (gain, w_qkv, w_out, *saved)],
        out_specs=[whole(array) for array in outs_shape],
        scratch_shapes=[
            pltpu.VMEM((total, sources), BF16),
            pltpu.VMEM((sources, total), BF16),
            pltpu.VMEM((sources, width), BF16),
            pltpu.VMEM((total, width), BF16),
            pltpu.VMEM((total, width), BF16),
            pltpu.VMEM((WINDOW, 2 * width), F32),
            pltpu.VMEM((width, WINDOW), F32),
            pltpu.VMEM((width, WINDOW), BF16),
            pltpu.VMEM((width, 3 * width), F32),
            pltpu.VMEM((width, width), F32),
            pltpu.VMEM((8, width), F32),
        ],
        compiler_params=PARAMS,
        cost_estimate=pl.CostEstimate(
            flops=20 << 30, bytes_accessed=8 << 20, transcendentals=4 << 20
        ),
        name="window_backward",
    )(rel, pattern, order, grads, *arrivals, *labels, gain, w_qkv, w_out, *saved)
    return outs[0], outs[1:5], outs[5]


def scale_sums(sums, factor, width):
    return pl.pallas_call(
        functools.partial(scale_kernel, factor),
        out_shape=[
            shape_of(1, width, dtype=F32),
            shape_of(width, 3 * width, dtype=F32),
            shape_of(width, width, dtype=F32),
        ],
        in_specs=[VMEM],
        out_specs=[VMEM] * 3,
        compiler_params=PARAMS,
        cost_estimate=pl.CostEstimate(flops=0, bytes_accessed=2 << 20, transcendentals=0),
        name="scale_sums",
    )(sums)


def shift_seq(array, by):
    peers = lax.axis_size("seq")
    pairs = [(i, i + by) for i in range(peers) if 0 <= i + by < peers]
    return lax.ppermute(array, "seq", pairs)


def exchange(arrays, sign):
    return [shift_seq(array, sign * by) for array, by in zip(arrays, DISTANCES)]


def swap_seq(array, bit):
    peers = lax.axis_size("seq")
    return lax.ppermute(array, "seq", [(i, i ^ bit) for i in range(peers)])


def swap_core(array):
    return lax.ppermute(array, "batch", [(0, 1), (1, 0)])


def split_half(array, upper):
    half = array.shape[0] // 2
    mine = lax.dynamic_slice_in_dim(array, upper * half, half)
    other = lax.dynamic_slice_in_dim(array, (1 - upper) * half, half)
    return mine, other


def join_half(mine, other, upper):
    low = jnp.where(upper == 0, mine, other)
    high = jnp.where(upper == 0, other, mine)
    return jnp.concatenate([low, high], axis=0)


def sum_everywhere(pieces):
    core = lax.axis_index("batch")
    here = lax.axis_index("seq")
    mine, other = split_half(pieces, core)
    part = mine + swap_core(other)
    bits = []
    for bit in (1, 2):
        upper = (here // bit) % 2
        bits.append((bit, upper))
        mine, other = split_half(part, upper)
        part = mine + swap_seq(other, bit)
    bit = 4
    while bit < lax.axis_size("seq"):
        part = part + swap_seq(part, bit)
        bit *= 2
    for bit, upper in reversed(bits):
        part = join_half(part, swap_seq(part, bit), upper)
    return join_half(part, swap_core(part), core)


def body(points, gain, w_qkv, w_out, route, order, pattern, grad_out):
    rows, grads = points[0], grad_out[0]
    total, width = rows.shape
    amount = total // SLOT
    rel = route[0] - lax.axis_index("seq") * amount
    order_row = order[0]
    seen = pattern.reshape(-1)
    gain_row = gain.reshape(1, width)
    point_packs, grad_packs = pack(rel, rows, grads)
    point_in = exchange(point_packs, 1)
    grad_in = exchange(grad_packs, 1)
    local, backs, saved = forward(
        rel, seen, order_row, rows, point_in, gain_row, w_qkv, w_qkv.T, w_out
    )
    out_back = exchange(backs, -1)
    d_local, d_backs, sums = backward(
        rel, seen, order_row, grads, grad_in, point_in, gain_row, w_qkv, w_out, saved
    )
    result = restore(rel, local, out_back)
    d_back = exchange(d_backs, -1)
    sums = sum_everywhere(sums)
    grad_points = restore(rel, d_local, d_back)
    factor = (lax.axis_size("batch") * lax.axis_size("seq") * total) ** (-0.5)
    g_gain, g_qkv, g_out = scale_sums(sums, factor, width)
    return (result[None], grad_points[None], g_gain.reshape(width), g_qkv, g_out)


def solution(mesh):
    return jax.shard_map(
        body,
        mesh=mesh,
        in_specs=(
            P("batch", "seq", None),
            P(),
            P(),
            P(),
            P("batch", "seq"),
            P("batch", "seq", None),
            P("batch", "seq", None, None),
            P("batch", "seq", None),
        ),
        out_specs=(P("batch", "seq", None), P("batch", "seq", None), P(), P(), P()),
        check_vma=False,
    )
```

```python
import functools

import jax
import jax.numpy as jnp
from jax import lax
from jax.experimental import pallas as pl
from jax.experimental.pallas import tpu as pltpu
from jax.sharding import PartitionSpec as P

HEADS = 8
WINDOW = 512
SLOT = 128
BLK = WINDOW // SLOT
CHANNELS = 4
MOST = 2
CORES, AROUND_X, AROUND_Y, AROUND_Z = 2, 4, 4, 8
PIECE = 32
LABEL_ROWS = 16
EPSILON = 1e-05
LOG2E = 1.4426950408889634

BF16 = jnp.bfloat16
F32 = jnp.float32


def dot(left, right):
    return lax.dot_general(left, right, (((1,), (0,)), ((), ())), preferred_element_type=F32)


def dot_nt(left, right):
    return lax.dot_general(left, right, (((1,), (1,)), ((), ())), preferred_element_type=F32)


def dot_tn(left, right):
    return lax.dot_general(left, right, (((0,), (0,)), ((), ())), preferred_element_type=F32)


def partner_of(device, channel):
    if channel == 0:
        return device ^ 1
    if channel == 1:
        return ((device + 1) ^ 1) - 1
    if channel == 2:
        return device ^ 2
    return ((device + 2) ^ 2) - 2


def slot_moves(route_ref, amount):
    here = lax.axis_index("seq")
    moves = []
    for s in range(amount):
        value = route_ref[s]
        moves.append((lax.div(value, amount) - here, lax.rem(value, amount)))
    return moves, [partner_of(here, channel) - here for channel in range(CHANNELS)]


def pack_kernel(route_ref, points_ref, grads_ref, *outs):
    amount = points_ref.shape[0] // SLOT
    width = points_ref.shape[1]
    moves, distances = slot_moves(route_ref, amount)
    point_outs, grad_outs = outs[:4], outs[4:]
    lane = lax.broadcasted_iota(jnp.int32, (LABEL_ROWS, width), 1)
    for out in outs:
        out[...] = jnp.zeros_like(out)
    for point_out, grad_out, distance in zip(point_outs, grad_outs, distances):
        count = jnp.int32(0)
        first = jnp.int32(0)
        second = jnp.int32(0)
        for s, (offset, spot) in enumerate(moves):
            goes = offset == distance

            @pl.when(goes)
            def _(s=s, count=count):
                start = pl.multiple_of(jnp.minimum(count, MOST - 1) * SLOT, SLOT)
                point_out[pl.ds(start, SLOT), :] = points_ref[s * SLOT : (s + 1) * SLOT, :]
                grad_out[pl.ds(start, SLOT), :] = grads_ref[s * SLOT : (s + 1) * SLOT, :]

            first = jnp.where(goes & (count == 0), spot + 1, first)
            second = jnp.where(goes & (count == 1), spot + 1, second)
            count = count + goes.astype(jnp.int32)
        labels = jnp.where(lane < SLOT, first, second).astype(F32).astype(BF16)
        point_out[MOST * SLOT :, :] = labels


def restore_kernel(route_ref, local_ref, *refs):
    arrivals, out_ref = refs[:4], refs[4]
    amount = local_ref.shape[0] // SLOT
    moves, distances = slot_moves(route_ref, amount)
    counts = [jnp.int32(0)] * 4
    for s, (offset, _) in enumerate(moves):
        rows = slice(s * SLOT, (s + 1) * SLOT)

        @pl.when(offset == 0)
        def _(rows=rows):
            out_ref[rows, :] = local_ref[rows, :]

        for number, distance in enumerate(distances):
            goes = offset == distance

            @pl.when(goes)
            def _(rows=rows, number=number, count=counts[number]):
                start = pl.multiple_of(jnp.minimum(count, MOST - 1) * SLOT, SLOT)
                out_ref[rows, :] = arrivals[number][pl.ds(start, SLOT), :]

            counts[number] = counts[number] + goes.astype(jnp.int32)


def landing_rows(route_ref, label_refs, amount):
    rows = []
    for offset, spot in slot_moves(route_ref, amount)[0]:
        landing = jnp.where(offset == 0, spot, -1) * SLOT
        rows.append(jnp.full((1, SLOT), landing, jnp.int32))
    for label in label_refs:
        held = label[0:1, :].astype(F32).astype(jnp.int32)
        for number in range(MOST):
            rows.append((held[:, number * SLOT : (number + 1) * SLOT] - 1) * SLOT)
    return rows


def order_columns(order_ref, column_ref):
    total = order_ref.shape[1]
    order = jnp.broadcast_to(order_ref[...].astype(F32), (SLOT, total))
    column_ref[...] = jnp.transpose(order).astype(jnp.int32)


def gather_window(column, rows, source_ref, place_ref):
    lane = lax.broadcasted_iota(jnp.int32, (1, SLOT), 1)
    for number, row in enumerate(rows):
        place_ref[:, number * SLOT : (number + 1) * SLOT] = (
            jnp.where(column == row + lane, 1.0, 0.0).astype(BF16)
        )
    return dot(place_ref[...], source_ref[...]).astype(BF16)


def scatter_rows(order_ref, rows, hilbert_ref, rows_ref, spread_ref, moved_ref, targets):
    total = order_ref.shape[1]
    rows_ref[...] = jnp.concatenate(rows, axis=0)

    @pl.loop(0, len(rows) // BLK)
    def _(quarter):
        inside = lax.broadcasted_iota(jnp.int32, (SLOT, total), 0)
        for number in range(BLK):
            row = rows_ref[pl.ds(quarter * BLK + number, 1), :]
            wide = jnp.concatenate([row] * (total // SLOT), axis=1)
            spread_ref[number * SLOT : (number + 1) * SLOT, :] = (
                jnp.where(order_ref[...] - wide == inside, 1.0, 0.0).astype(BF16)
            )
        span = pl.ds(pl.multiple_of(quarter * WINDOW, WINDOW), WINDOW)
        moved_ref[span, :] = dot(spread_ref[...], hilbert_ref[...]).astype(BF16)

    start = 0
    for target in targets:
        amount = target.shape[0]
        target[...] = moved_ref[start : start + amount, :]
        start += amount


def bias_rows(pattern_ref, window):
    rows = []
    for key_block in range(BLK):
        pieces = []
        for query_block in range(BLK):
            if query_block == key_block:
                pieces.append(jnp.zeros((1, SLOT), F32))
            else:
                seen = pattern_ref[window * BLK * BLK + query_block * BLK + key_block] > 0
                pieces.append(jnp.full((1, SLOT), jnp.where(seen, 0.0, -jnp.inf), F32))
        rows.append(jnp.concatenate(pieces, axis=1))
    return rows


def by_block(rows):
    return jnp.concatenate([row[None] for row in rows], axis=0)


def norm_stats(rows):
    as_float = rows.astype(F32)
    centred = as_float - jnp.mean(as_float, axis=-1, keepdims=True)
    inverse_std = lax.rsqrt(jnp.mean(centred * centred, axis=-1, keepdims=True) + EPSILON)
    return as_float, centred * inverse_std, inverse_std


def forward_kernel(
    route_ref,
    pattern_ref,
    order_ref,
    points_ref,
    a0,
    a1,
    a2,
    a3,
    gain_ref,
    w_qkv_ref,
    w_qkv_t_ref,
    w_out_ref,
    local_ref,
    r0,
    r1,
    r2,
    r3,
    hilbert_ref,
    qkv_ref,
    qk_t_ref,
    mixed_t_ref,
    lse_ref,
    column_ref,
    place_ref,
    rows_ref,
    source_ref,
    v_t_ref,
    out_ref,
):
    arrivals = (a0, a1, a2, a3)
    total, width = points_ref.shape
    head_dim = width // HEADS
    factor = head_dim ** (-0.5) * LOG2E
    source_ref[0:total, :] = points_ref[...]
    for number, arrival in enumerate(arrivals):
        start = total + number * MOST * SLOT
        source_ref[start : start + MOST * SLOT, :] = arrival[0 : MOST * SLOT, :]
    labels = [arrival.at[MOST * SLOT : MOST * SLOT + LABEL_ROWS] for arrival in arrivals]
    rows = landing_rows(route_ref, labels, total // SLOT)
    order_columns(order_ref, column_ref)

    @pl.loop(0, total // WINDOW)
    def _(window):
        span = pl.ds(pl.multiple_of(window * WINDOW, WINDOW), WINDOW)
        h = gather_window(column_ref[span, :], rows, source_ref, place_ref)
        hilbert_ref[span, :] = h
        as_float, normalized, _ = norm_stats(h)
        normed = (normalized * gain_ref[...]).astype(BF16)
        qkv = dot(normed, w_qkv_ref[...]).astype(BF16)
        qkv_ref[span, :] = qkv
        qkv_t = dot_nt(w_qkv_t_ref[...], normed).astype(BF16)
        qk_t_ref[window] = qkv_t[: 2 * width]
        v_t_ref[...] = qkv_t[2 * width :]
        bias = by_block(bias_rows(pattern_ref, window))
        for head in range(HEADS):
            low = head * head_dim
            keys = qkv_ref[span, width + low : width + low + head_dim]
            queries_t = qk_t_ref[window, low : low + head_dim, :]
            scores = dot(keys, queries_t).reshape(BLK, SLOT, WINDOW) + bias
            highest = jnp.max(scores, axis=(0, 1), keepdims=True)
            powers = jnp.exp2((scores - highest) * factor)
            total_power = jnp.sum(powers, axis=(0, 1), keepdims=True)
            probs = (powers * (1.0 / total_power)).astype(BF16).reshape(WINDOW, WINDOW)
            mixed_t = dot(v_t_ref[low : low + head_dim, :], probs)
            mixed_t_ref[window, low : low + head_dim, :] = mixed_t.astype(BF16)
            lse = highest * factor + jnp.log2(total_power)
            lse_ref[window, head : head + 1, :] = lse.reshape(1, WINDOW)
        mixed = jnp.transpose(mixed_t_ref[window])
        out_ref[span, :] = (as_float + dot(mixed, w_out_ref[...])).astype(BF16)

    scatter_rows(
        order_ref,
        rows,
        out_ref,
        rows_ref,
        place_ref.at[:, 0:total],
        source_ref,
        (local_ref, r0, r1, r2, r3),
    )


def backward_kernel(
    route_ref,
    pattern_ref,
    order_ref,
    grads_ref,
    a0,
    a1,
    a2,
    a3,
    l0,
    l1,
    l2,
    l3,
    gain_ref,
    w_qkv_ref,
    w_out_ref,
    hilbert_ref,
    qkv_ref,
    qk_t_ref,
    mixed_t_ref,
    lse_ref,
    d_qkv_ref,
    upstream_ref,
    own_ref,
    other_ref,
    column_ref,
    place_ref,
    source_ref,
    d_kv_ref,
    d_q_t_ref,
    d_mixed_t_ref,
    g_qkv_ref,
    g_out_ref,
    g_gain_ref,
):
    arrivals = (a0, a1, a2, a3)
    total, width = grads_ref.shape
    head_dim = width // HEADS
    scale = head_dim ** (-0.5)
    factor = scale * LOG2E
    source_ref[0:total, :] = grads_ref[...]
    for number, arrival in enumerate(arrivals):
        start = total + number * MOST * SLOT
        source_ref[start : start + MOST * SLOT, :] = arrival[...]
    rows = landing_rows(route_ref, (l0, l1, l2, l3), total // SLOT)
    order_columns(order_ref, column_ref)
    g_qkv_ref[...] = jnp.zeros_like(g_qkv_ref)
    g_out_ref[...] = jnp.zeros_like(g_out_ref)
    g_gain_ref[...] = jnp.zeros_like(g_gain_ref)

    @pl.loop(0, total // WINDOW)
    def _(window):
        span = pl.ds(pl.multiple_of(window * WINDOW, WINDOW), WINDOW)
        upstream = gather_window(column_ref[span, :], rows, source_ref, place_ref)
        upstream_ref[span, :] = upstream
        g_out_ref[...] += dot(mixed_t_ref[window], upstream)
        d_mixed = dot_nt(upstream, w_out_ref[...]).astype(BF16)
        d_mixed_t_ref[...] = dot_nt(w_out_ref[...], upstream).astype(BF16)
        bias = by_block(bias_rows(pattern_ref, window))
        for head in range(HEADS):
            low = head * head_dim
            high = low + head_dim
            queries = qkv_ref[span, low:high]
            keys = qkv_ref[span, width + low : width + high]
            values = qkv_ref[span, 2 * width + low : 2 * width + high]
            queries_t = qk_t_ref[window, low:high, :]
            keys_t = qk_t_ref[window, width + low : width + high, :]
            shift = bias - lse_ref[window, head : head + 1, :].reshape(1, 1, WINDOW)
            scores = dot(keys, queries_t).reshape(BLK, SLOT, WINDOW)
            probs = jnp.exp2(scores * factor + shift).reshape(WINDOW, WINDOW)
            d_block = d_mixed[:, low:high]
            d_values = dot(probs.astype(BF16), d_block)
            d_probs = dot(values, d_mixed_t_ref[low:high, :])
            inner = jnp.sum(d_probs * probs, axis=0, keepdims=True)
            d_scores = (probs * (d_probs - inner) * scale).astype(BF16)
            d_keys = dot(d_scores, queries)
            d_q_t_ref[low:high, :] = dot(keys_t, d_scores)
            d_kv_ref[:, low:high] = d_keys
            d_kv_ref[:, width + low : width + high] = d_values
        d_q = jnp.transpose(d_q_t_ref[...])
        d_qkv = jnp.concatenate([d_q, d_kv_ref[...]], axis=1).astype(BF16)
        d_qkv_ref[span, :] = d_qkv
        _, normalized, _ = norm_stats(hilbert_ref[span, :])
        normed = (normalized * gain_ref[...]).astype(BF16)
        g_qkv_ref[...] += dot_tn(normed, d_qkv)
        d_normed = dot_nt(d_qkv, w_qkv_ref[...])
        g_gain_ref[0:1, :] += jnp.sum(d_normed * normalized, axis=0, keepdims=True)

    core, x, y = places()
    spread = AROUND_Y * PIECE
    for half, target in enumerate((own_ref, other_ref)):
        for start in range(AROUND_X):
            target[start, spread : spread + 8, :] = g_gain_ref[...]
        for number in range(AROUND_X * AROUND_Y):
            for side in range(CORES):
                row = (side * AROUND_X * AROUND_Y + number) * PIECE
                block, inside = row // width, row % width
                to_x = (number // AROUND_Y) ^ x
                to_y = pl.multiple_of(((number % AROUND_Y) ^ y) * PIECE, PIECE)

                @pl.when(core == side ^ half)
                def _(target=target, block=block, inside=inside, to_x=to_x, to_y=to_y):
                    if block < 3:
                        piece = g_qkv_ref[
                            inside : inside + PIECE, block * width : (block + 1) * width
                        ]
                    else:
                        piece = g_out_ref[inside : inside + PIECE, :]
                    target[to_x, pl.ds(to_y, PIECE), :] = piece


def places():
    here = lax.axis_index("seq")
    return lax.axis_index("batch"), lax.rem(here, AROUND_X), lax.div(here, AROUND_X * AROUND_Z)


def input_grad_kernel(
    route_ref,
    order_ref,
    l0,
    l1,
    l2,
    l3,
    gain_ref,
    w_qkv_ref,
    hilbert_ref,
    d_qkv_ref,
    upstream_ref,
    local_ref,
    r0,
    r1,
    r2,
    r3,
    rows_ref,
    spread_ref,
    moved_ref,
    d_rows_ref,
):
    total, width = hilbert_ref.shape
    rows = landing_rows(route_ref, (l0, l1, l2, l3), total // SLOT)

    @pl.loop(0, total // WINDOW)
    def _(window):
        span = pl.ds(pl.multiple_of(window * WINDOW, WINDOW), WINDOW)
        _, normalized, inverse_std = norm_stats(hilbert_ref[span, :])
        d_hat = dot_nt(d_qkv_ref[span, :], w_qkv_ref[...]) * gain_ref[...]
        branch = inverse_std * (
            d_hat
            - jnp.mean(d_hat, axis=-1, keepdims=True)
            - normalized * jnp.mean(d_hat * normalized, axis=-1, keepdims=True)
        )
        d_rows_ref[span, :] = (upstream_ref[span, :].astype(F32) + branch).astype(BF16)

    scatter_rows(
        order_ref, rows, d_rows_ref, rows_ref, spread_ref, moved_ref, (local_ref, r0, r1, r2, r3)
    )


def scale_kernel(factor, gain_sum_ref, own_ref, other_ref, gain_ref, qkv_ref, out_ref):
    width = out_ref.shape[1]
    core, x, y = places()
    for half, source in enumerate((own_ref, other_ref)):
        for number in range(AROUND_X * AROUND_Y):
            from_x = (number // AROUND_Y) ^ x
            from_y = (number % AROUND_Y) ^ y
            start = pl.multiple_of((from_x * AROUND_Y + from_y) * PIECE, PIECE)
            piece = source[pl.ds(start, PIECE), :] * factor
            for side in range(CORES):
                row = (side * AROUND_X * AROUND_Y + number) * PIECE
                block, inside = row // width, row % width

                @pl.when(core == side ^ half)
                def _(piece=piece, block=block, inside=inside):
                    if block < 3:
                        cols = slice(block * width, (block + 1) * width)
                        qkv_ref[inside : inside + PIECE, cols] = piece
                    else:
                        out_ref[inside : inside + PIECE, :] = piece
    gain_ref[...] = gain_sum_ref[0:1, :] * factor


VMEM = pl.BlockSpec(memory_space=pltpu.VMEM)
SMEM = pl.BlockSpec(memory_space=pltpu.SMEM)


def params(mebibytes):
    return pltpu.CompilerParams(vmem_limit_bytes=mebibytes << 20)


def shape_of(*dims, dtype=BF16):
    return jax.ShapeDtypeStruct(dims, dtype)


def label_spec(width):
    return pl.BlockSpec((LABEL_ROWS, width), lambda i: (MOST * SLOT // LABEL_ROWS, 0))


def whole(array):
    return pl.BlockSpec(array.shape, lambda i: (0,) * array.ndim)


def pack(route, points, grads):
    width = points.shape[1]
    tall = MOST * SLOT + LABEL_ROWS
    outs = pl.pallas_call(
        pack_kernel,
        out_shape=[shape_of(tall, width)] * 4 + [shape_of(MOST * SLOT, width)] * 4,
        in_specs=[SMEM, VMEM, VMEM],
        out_specs=[VMEM] * 8,
        compiler_params=params(8),
        cost_estimate=pl.CostEstimate(flops=0, bytes_accessed=2 << 20, transcendentals=0),
        name="pack_slots",
    )(route, points, grads)
    return outs[:4], outs[4:]


def restore(route, local, arrivals):
    return pl.pallas_call(
        restore_kernel,
        out_shape=shape_of(*local.shape),
        in_specs=[SMEM] + [VMEM] * 5,
        out_specs=VMEM,
        compiler_params=params(8),
        cost_estimate=pl.CostEstimate(flops=0, bytes_accessed=3 << 19, transcendentals=0),
        name="restore_slots",
    )(route, local, *arrivals)


def forward(route, pattern, order, points, arrivals, gain, w_qkv, w_qkv_t, w_out):
    total, width = points.shape
    windows = total // WINDOW
    sources = total + 4 * MOST * SLOT
    outs = pl.pallas_call(
        forward_kernel,
        out_shape=[shape_of(total, width)]
        + [shape_of(MOST * SLOT, width)] * 4
        + [
            shape_of(total, width),
            shape_of(total, 3 * width),
            shape_of(windows, 2 * width, WINDOW),
            shape_of(windows, width, WINDOW),
            shape_of(windows, HEADS, WINDOW, dtype=F32),
        ],
        in_specs=[SMEM, SMEM] + [VMEM] * 10,
        out_specs=[VMEM] * 10,
        scratch_shapes=[
            pltpu.VMEM((total, SLOT), jnp.int32),
            pltpu.VMEM((WINDOW, sources), BF16),
            pltpu.VMEM((sources // SLOT, SLOT), jnp.int32),
            pltpu.VMEM((sources, width), BF16),
            pltpu.VMEM((width, WINDOW), BF16),
            pltpu.VMEM((total, width), BF16),
        ],
        compiler_params=params(32),
        cost_estimate=pl.CostEstimate(
            flops=12 << 30, bytes_accessed=8 << 20, transcendentals=4 << 20
        ),
        name="window_forward",
    )(route, pattern, order, points, *arrivals, gain, w_qkv, w_qkv_t, w_out)
    return outs[0], outs[1:5], outs[5:]


def backward(route, pattern, order, grads, arrivals, labels, gain, w_qkv, w_out, saved):
    total, width = grads.shape
    sources = total + 4 * MOST * SLOT
    tall = AROUND_Y * PIECE + 8
    outs_shape = [
        shape_of(total, 3 * width),
        shape_of(total, width),
        shape_of(AROUND_X, tall, width, dtype=F32),
        shape_of(AROUND_X, tall, width, dtype=F32),
    ]
    return pl.pallas_call(
        backward_kernel,
        grid=(1,),
        out_shape=outs_shape,
        in_specs=[SMEM, SMEM]
        + [whole(array) for array in (order, grads, *arrivals)]
        + [label_spec(width)] * 4
        + [whole(array) for array in (gain, w_qkv, w_out, *saved)],
        out_specs=[whole(array) for array in outs_shape],
        scratch_shapes=[
            pltpu.VMEM((total, SLOT), jnp.int32),
            pltpu.VMEM((WINDOW, sources), BF16),
            pltpu.VMEM((sources, width), BF16),
            pltpu.VMEM((WINDOW, 2 * width), F32),
            pltpu.VMEM((width, WINDOW), F32),
            pltpu.VMEM((width, WINDOW), BF16),
            pltpu.VMEM((width, 3 * width), F32),
            pltpu.VMEM((width, width), F32),
            pltpu.VMEM((8, width), F32),
        ],
        compiler_params=params(36),
        cost_estimate=pl.CostEstimate(
            flops=20 << 30, bytes_accessed=8 << 20, transcendentals=4 << 20
        ),
        name="window_backward",
    )(route, pattern, order, grads, *arrivals, *labels, gain, w_qkv, w_out, *saved)


def input_grad(route, order, labels, gain, w_qkv, hilbert, d_qkv, upstream):
    total, width = hilbert.shape
    sources = total + 4 * MOST * SLOT
    outs_shape = [shape_of(total, width)] + [shape_of(MOST * SLOT, width)] * 4
    outs = pl.pallas_call(
        input_grad_kernel,
        grid=(1,),
        out_shape=outs_shape,
        in_specs=[SMEM, whole(order)]
        + [label_spec(width)] * 4
        + [whole(array) for array in (gain, w_qkv, hilbert, d_qkv, upstream)],
        out_specs=[whole(array) for array in outs_shape],
        scratch_shapes=[
            pltpu.VMEM((sources // SLOT, SLOT), jnp.int32),
            pltpu.VMEM((WINDOW, total), BF16),
            pltpu.VMEM((sources, width), BF16),
            pltpu.VMEM((total, width), BF16),
        ],
        compiler_params=params(24),
        cost_estimate=pl.CostEstimate(
            flops=2 << 30, bytes_accessed=5 << 20, transcendentals=0
        ),
        name="input_grad",
    )(route, order, *labels, gain, w_qkv, hilbert, d_qkv, upstream)
    return outs[0], outs[1:]


def scale_sums(gain_sum, own, other, factor):
    width = own.shape[1]
    return pl.pallas_call(
        functools.partial(scale_kernel, factor),
        out_shape=[
            shape_of(1, width, dtype=F32),
            shape_of(width, 3 * width, dtype=F32),
            shape_of(width, width, dtype=F32),
        ],
        in_specs=[VMEM] * 3,
        out_specs=[VMEM] * 3,
        compiler_params=params(8),
        cost_estimate=pl.CostEstimate(flops=0, bytes_accessed=2 << 20, transcendentals=0),
        name="scale_sums",
    )(gain_sum, own, other)


def exchange(arrays):
    peers = lax.axis_size("seq")
    out = []
    for channel, array in enumerate(arrays):
        pairs = [(i, partner_of(i, channel)) for i in range(peers)]
        pairs = [(i, j) for i, j in pairs if 0 <= j < peers]
        out.append(lax.ppermute(array, "seq", pairs))
    return out


def swap_seq(array, bits):
    peers = lax.axis_size("seq")
    return lax.ppermute(array, "seq", [(i, i ^ bits) for i in range(peers)])


def swap_core(array):
    return lax.ppermute(array, "batch", [(0, 1), (1, 0)])


def four_way(pieces, step):
    came = [swap_seq(pieces[j], j * step) for j in (1, 2, 3)]
    return (pieces[0] + came[0]) + (came[1] + came[2])


def gather_four(piece, step):
    return jnp.concatenate([piece] + [swap_seq(piece, j * step) for j in (1, 2, 3)], axis=0)


def tie(wanted, first):
    return lax.optimization_barrier((wanted, first))


def body(points, gain, w_qkv, w_out, route, order, pattern, grad_out):
    rows, grads = points[0], grad_out[0]
    total, width = rows.shape
    route = route[0]
    order_row = order[0]
    seen = pattern.reshape(-1)
    gain_row = gain.reshape(1, width)
    point_packs, grad_packs = pack(route, rows, grads)
    point_in = exchange(point_packs)
    grad_in = exchange(grad_packs)
    local, backs, saved = forward(
        route, seen, order_row, rows, point_in, gain_row, w_qkv, w_qkv.T, w_out
    )
    out_back = exchange(backs)
    d_qkv, upstream, own, other = backward(
        route, seen, order_row, grads, grad_in, point_in, gain_row, w_qkv, w_out, saved
    )
    (own, other), out_back = tie((own, other), out_back)
    step_z, step_y = AROUND_X, AROUND_X * AROUND_Z
    spread = AROUND_Y * PIECE
    part = own + swap_core(other)
    d_local, d_backs = input_grad(
        route, order_row, point_in, gain_row, w_qkv, saved[0], d_qkv, upstream
    )
    part = four_way([part[j] for j in range(AROUND_X)], 1)
    part, (d_local, d_backs) = tie(part, (d_local, d_backs))
    d_back = exchange(d_backs)
    gain_rows = part[spread:]
    part = four_way(
        [
            jnp.concatenate([part[j * PIECE : (j + 1) * PIECE], gain_rows], axis=0)
            for j in range(AROUND_Y)
        ],
        step_y,
    )
    part = four_way([part] * 4, step_z)
    part = part + swap_seq(part, 4 * step_z)
    result = restore(route, local, out_back)
    part, (d_back, result) = tie(part, (d_back, result))
    gain_sum = part[PIECE:]
    part = gather_four(part[:PIECE], step_y)
    part = gather_four(part, 1)
    grad_points = restore(route, d_local, d_back)
    part, grad_points = tie(part, grad_points)
    own, other = part, swap_core(part)
    factor = (lax.axis_size("batch") * lax.axis_size("seq") * total) ** (-0.5)
    g_gain, g_qkv, g_out = scale_sums(gain_sum, own, other, factor)
    return (result[None], grad_points[None], g_gain.reshape(width), g_qkv, g_out)


def solution(mesh):
    return jax.shard_map(
        body,
        mesh=mesh,
        in_specs=(
            P("batch", "seq", None),
            P(),
            P(),
            P(),
            P("batch", "seq"),
            P("batch", "seq", None),
            P("batch", "seq", None, None),
            P("batch", "seq", None),
        ),
        out_specs=(P("batch", "seq", None), P("batch", "seq", None), P(), P(), P()),
        check_vma=False,
    )
```

```python
import functools

import jax
import jax.numpy as jnp
from jax import lax
from jax.experimental import pallas as pl
from jax.experimental.pallas import tpu as pltpu
from jax.sharding import PartitionSpec as P

HEADS = 8
WINDOW = 512
SLOT = 128
BLK = WINDOW // SLOT
CHANNELS = 4
MOST = 2
CORES, AROUND_X, AROUND_Y, AROUND_Z = 2, 4, 4, 8
PIECE = 32
CHUNK = 64
LABEL_ROWS = 16
EPSILON = 1e-05
LOG2E = 1.4426950408889634


BF16 = jnp.bfloat16
F32 = jnp.float32


def dot(left, right):
    return lax.dot_general(left, right, (((1,), (0,)), ((), ())), preferred_element_type=F32)


def dot_nt(left, right):
    return lax.dot_general(left, right, (((1,), (1,)), ((), ())), preferred_element_type=F32)


def dot_tn(left, right):
    return lax.dot_general(left, right, (((0,), (0,)), ((), ())), preferred_element_type=F32)


def partner_of(device, channel):
    if channel == 0:
        return device ^ 1
    if channel == 1:
        return ((device + 1) ^ 1) - 1
    if channel == 2:
        return device ^ 2
    return ((device + 2) ^ 2) - 2


def slot_moves(route_ref, amount):
    here = lax.axis_index("seq")
    moves = []
    for s in range(amount):
        value = route_ref[s]
        moves.append((lax.div(value, amount) - here, lax.rem(value, amount)))
    return moves, [partner_of(here, channel) - here for channel in range(CHANNELS)]


def fetch(sources, targets, sems):
    copies = [
        pltpu.make_async_copy(source, target, sems.at[number])
        for number, (source, target) in enumerate(zip(sources, targets))
    ]
    for copy in copies:
        copy.start()
    for copy in copies:
        copy.wait()


def pack_kernel(route_hbm, rows_hbm, *refs):
    outs, (route_ref, rows_ref, sems) = refs[:CHANNELS], refs[CHANNELS:]
    fetch((route_hbm, rows_hbm), (route_ref, rows_ref), sems)
    amount = rows_ref.shape[0] // SLOT
    width = rows_ref.shape[1]
    moves, distances = slot_moves(route_ref, amount)
    for out, distance in zip(outs, distances):
        out[...] = jnp.zeros_like(out)
        count = jnp.int32(0)
        first = jnp.int32(0)
        second = jnp.int32(0)
        for s, (offset, spot) in enumerate(moves):
            goes = offset == distance

            @pl.when(goes)
            def _(s=s, count=count):
                start = pl.multiple_of(jnp.minimum(count, MOST - 1) * SLOT, SLOT)
                out[pl.ds(start, SLOT), :] = rows_ref[s * SLOT : (s + 1) * SLOT, :]

            first = jnp.where(goes & (count == 0), spot + 1, first)
            second = jnp.where(goes & (count == 1), spot + 1, second)
            count = count + goes.astype(jnp.int32)
        if out.shape[0] > MOST * SLOT:
            lane = lax.broadcasted_iota(jnp.int32, (LABEL_ROWS, width), 1)
            labels = jnp.where(lane < SLOT, first, second).astype(F32).astype(BF16)
            out[MOST * SLOT :, :] = labels


def restore_kernel(route_ref, local_ref, *refs):
    arrivals, outs = refs[:CHANNELS], refs[CHANNELS:]
    amount = local_ref.shape[0] // SLOT
    width = outs[0].shape[1]
    moves, distances = slot_moves(route_ref, amount)
    counts = [jnp.int32(0)] * CHANNELS
    for s, (offset, _) in enumerate(moves):
        rows = slice(s * SLOT, (s + 1) * SLOT)

        def put(source, start):
            for number, out in enumerate(outs):
                cols = slice(number * width, (number + 1) * width)
                out[rows, :] = source[pl.ds(start, SLOT), cols]

        @pl.when(offset == 0)
        def _(put=put, s=s):
            put(local_ref, s * SLOT)

        for number, distance in enumerate(distances):
            goes = offset == distance

            @pl.when(goes)
            def _(put=put, number=number, count=counts[number]):
                put(
                    arrivals[number],
                    pl.multiple_of(jnp.minimum(count, MOST - 1) * SLOT, SLOT),
                )

            counts[number] = counts[number] + goes.astype(jnp.int32)


def read_landings(arrivals, landing_ref):
    for channel, arrival in enumerate(arrivals):
        label = arrival[MOST * SLOT : MOST * SLOT + LABEL_ROWS, :].astype(F32)
        for number in range(MOST):
            held = jnp.max(label[0:8, number * SLOT : (number + 1) * SLOT])
            landing_ref[channel * MOST + number] = held.astype(jnp.int32) - 1


def arrive(route_ref, landing_ref, own_ref, arrivals, arrived_ref):
    amount = own_ref.shape[0] // SLOT

    def put(source, start, landing):
        to = pl.ds(pl.multiple_of(landing * SLOT, SLOT), SLOT)
        arrived_ref[to, :] = source[start : start + SLOT, :]

    for s, (offset, spot) in enumerate(slot_moves(route_ref, amount)[0]):

        @pl.when(offset == 0)
        def _(s=s, spot=spot):
            put(own_ref, s * SLOT, spot)

    for channel, arrival in enumerate(arrivals):
        for number in range(MOST):
            landing = landing_ref[channel * MOST + number]

            @pl.when(landing >= 0)
            def _(arrival=arrival, number=number, landing=landing):
                put(arrival, number * SLOT, jnp.minimum(landing, amount - 1))


def leave(route_ref, landing_ref, moved_ref, local_ref, backs):
    amount = local_ref.shape[0] // SLOT

    def take(target, start, landing):
        at = pl.ds(pl.multiple_of(landing * SLOT, SLOT), SLOT)
        target[start : start + SLOT, :] = moved_ref[at, :]

    for s, (offset, spot) in enumerate(slot_moves(route_ref, amount)[0]):

        @pl.when(offset == 0)
        def _(s=s, spot=spot):
            take(local_ref, s * SLOT, spot)

    for channel, back in enumerate(backs):
        for number in range(MOST):
            landing = landing_ref[channel * MOST + number]

            @pl.when(landing >= 0)
            def _(back=back, number=number, landing=landing):
                take(back, number * SLOT, jnp.minimum(landing, amount - 1))


def order_columns(order_ref, column_ref):
    total = order_ref.shape[1]
    order = jnp.broadcast_to(order_ref[...].astype(F32), (SLOT, total))
    column_ref[...] = jnp.transpose(order).astype(jnp.int32)


def gather_window(column, arrived_ref, place_ref):
    lane = lax.broadcasted_iota(jnp.int32, (1, SLOT), 1)
    for start in range(0, arrived_ref.shape[0], SLOT):
        place_ref[:, start : start + SLOT] = (
            jnp.where(column == lane + start, 1.0, 0.0).astype(BF16)
        )
    return dot(place_ref[...], arrived_ref[...]).astype(BF16)


def scatter_rows(order_ref, hilbert_ref, spread_ref, moved_ref):
    total = order_ref.shape[1]

    @pl.loop(0, total // WINDOW)
    def _(part):
        inside = lax.broadcasted_iota(jnp.int32, (WINDOW, total), 0) + part * WINDOW
        spread_ref[...] = jnp.where(order_ref[...] == inside, 1.0, 0.0).astype(BF16)
        span = pl.ds(pl.multiple_of(part * WINDOW, WINDOW), WINDOW)
        moved_ref[span, :] = dot(spread_ref[...], hilbert_ref[...]).astype(BF16)


def bias_rows(pattern_ref, window):
    rows = []
    for key_block in range(BLK):
        pieces = []
        for query_block in range(BLK):
            if query_block == key_block:
                pieces.append(jnp.zeros((8, SLOT), F32))
            else:
                seen = pattern_ref[window, query_block, key_block] > 0
                pieces.append(jnp.full((8, SLOT), jnp.where(seen, 0.0, -jnp.inf), F32))
        rows.append(jnp.concatenate(pieces, axis=1))
    return rows


def interleave(work):
    last = {}
    going = dict(work)
    while going:
        for key, steps in list(going.items()):
            try:
                last[key] = next(steps)
            except StopIteration:
                del going[key]
    return last


def by_block(rows):
    return jnp.concatenate([row[None] for row in rows], axis=0)


def tiles(array):
    return array.reshape(array.shape[0] // 8, 8, array.shape[1])


def spread_rows(row):
    return jnp.broadcast_to(row, (8, row.shape[1]))


def norm_stats(rows):
    as_float = rows.astype(F32)
    centred = as_float - jnp.mean(as_float, axis=-1, keepdims=True)
    inverse_std = lax.rsqrt(jnp.mean(centred * centred, axis=-1, keepdims=True) + EPSILON)
    return as_float, centred * inverse_std, inverse_std


def forward_kernel(
    route_hbm,
    pattern_hbm,
    order_hbm,
    points_hbm,
    gain_hbm,
    w_qkv_hbm,
    w_out_hbm,
    a0,
    a1,
    a2,
    a3,
    out_ref,
    hilbert_ref,
    qkv_ref,
    qk_t_ref,
    mixed_t_ref,
    lse_ref,
    landing_ref,
    route_ref,
    pattern_ref,
    order_ref,
    gain_ref,
    w_qkv_ref,
    w_out_ref,
    sems,
    points_ref,
    column_ref,
    place_ref,
    source_ref,
    v_t_ref,
    w_qkv_t_ref,
    held_ref,
    probs_ref,
):
    arrivals = (a0, a1, a2, a3)
    total, width = points_hbm.shape
    head_dim = width // HEADS
    factor = head_dim ** (-0.5) * LOG2E
    fetch(
        (order_hbm, w_qkv_hbm, route_hbm, pattern_hbm, points_hbm, gain_hbm, w_out_hbm),
        (
            order_ref,
            w_qkv_ref,
            route_ref,
            pattern_ref,
            points_ref,
            gain_ref,
            w_out_ref,
        ),
        sems,
    )
    read_landings(arrivals, landing_ref)
    arrive(route_ref, landing_ref, points_ref, arrivals, source_ref)
    order_columns(order_ref, column_ref)
    w_qkv_t_ref[...] = jnp.transpose(w_qkv_ref[...])

    @pl.loop(0, total // WINDOW)
    def _(window):
        span = pl.ds(pl.multiple_of(window * WINDOW, WINDOW), WINDOW)
        h = gather_window(column_ref[span, :], source_ref, place_ref)
        hilbert_ref[span, :] = h
        as_float, normalized, _ = norm_stats(h)
        normed = (normalized * gain_ref[...]).astype(BF16)
        qkv = dot(normed, w_qkv_ref[...]).astype(BF16)
        qkv_ref[span, :] = qkv
        qkv_t = dot_nt(w_qkv_t_ref[...], normed).astype(BF16)
        qk_t_ref[window] = qkv_t[: 2 * width]
        v_t_ref[...] = qkv_t[2 * width :]
        bias = bias_rows(pattern_ref, window)

        def score(head, held):
            low = head * head_dim
            top = jnp.full((8, WINDOW), -jnp.inf, F32)
            for start in range(0, WINDOW, CHUNK):
                rows_at = pl.ds(pl.multiple_of(window * WINDOW + start, CHUNK), CHUNK)
                keys = qkv_ref[rows_at, width + low : width + low + head_dim]
                scores = dot(keys, qk_t_ref[window, low : low + head_dim, :])
                scores = tiles(scores) + bias[start // SLOT][None]
                held[start : start + CHUNK, :] = scores.reshape(CHUNK, WINDOW)
                top = jnp.maximum(top, jnp.max(scores, axis=0))
                yield None
            yield jnp.max(top, axis=0, keepdims=True)

        def power(highest, held):
            highest = spread_rows(highest * factor)
            total_power = jnp.zeros((8, WINDOW), F32)
            for start in range(0, WINDOW, CHUNK):
                scores = tiles(held[start : start + CHUNK, :])
                powers = jnp.exp2(scores * factor - highest[None])
                held[start : start + CHUNK, :] = powers.reshape(CHUNK, WINDOW)
                total_power += jnp.sum(powers, axis=0)
                yield None
            yield jnp.sum(total_power, axis=0, keepdims=True)

        def share(head, highest, total_power, held):
            low = head * head_dim
            inverse = spread_rows(1.0 / total_power)
            for start in range(0, WINDOW, CHUNK):
                probs = tiles(held[start : start + CHUNK, :]) * inverse[None]
                probs_ref[head % 2, start : start + CHUNK, :] = (
                    probs.reshape(CHUNK, WINDOW).astype(BF16)
                )
                yield None
            mixed_t = dot(v_t_ref[low : low + head_dim, :], probs_ref[head % 2])
            mixed_t_ref[window, low : low + head_dim, :] = mixed_t.astype(BF16)
            lse_ref[window, head : head + 1, :] = highest * factor + jnp.log2(total_power)
            yield None

        scored = {}
        powered = {}
        for step in range(HEADS + 2):
            work = {}
            if step < HEADS:
                work[0] = score(step, held_ref.at[step % 3])
            if 0 <= step - 1 < HEADS:
                work[1] = power(scored[step - 1], held_ref.at[(step - 1) % 3])
            if 0 <= step - 2 < HEADS:
                work[2] = share(
                    step - 2, scored[step - 2], powered[step - 2], held_ref.at[(step - 2) % 3]
                )
            last = interleave(work)
            if 0 in last:
                scored[step] = last[0]
            if 1 in last:
                powered[step - 1] = last[1]
        mixed = jnp.transpose(mixed_t_ref[window])
        out_ref[span, :] = (as_float + dot(mixed, w_out_ref[...])).astype(BF16)


def backward_kernel(
    route_ref,
    landing_ref,
    pattern_ref,
    order_ref,
    grads_ref,
    a0,
    a1,
    a2,
    a3,
    gain_ref,
    w_qkv_ref,
    w_out_ref,
    hilbert_ref,
    qkv_ref,
    qk_t_ref,
    mixed_t_ref,
    lse_ref,
    d_qkv_ref,
    upstream_ref,
    own_ref,
    other_ref,
    column_ref,
    place_ref,
    source_ref,
    d_qkv_t_ref,
    d_mixed_t_ref,
    g_qkv_t_ref,
    g_out_ref,
    g_gain_ref,
):
    arrivals = (a0, a1, a2, a3)
    total, width = grads_ref.shape
    head_dim = width // HEADS
    scale = head_dim ** (-0.5)
    factor = scale * LOG2E
    arrive(route_ref, landing_ref, grads_ref, arrivals, source_ref)
    order_columns(order_ref, column_ref)
    g_qkv_t_ref[...] = jnp.zeros_like(g_qkv_t_ref)
    g_out_ref[...] = jnp.zeros_like(g_out_ref)
    g_gain_ref[...] = jnp.zeros_like(g_gain_ref)

    @pl.loop(0, total // WINDOW)
    def _(window):
        span = pl.ds(pl.multiple_of(window * WINDOW, WINDOW), WINDOW)
        upstream = gather_window(column_ref[span, :], source_ref, place_ref)
        upstream_ref[span, :] = upstream
        g_out_ref[...] += dot(mixed_t_ref[window], upstream)
        d_mixed_t_ref[...] = dot_nt(w_out_ref[...], upstream).astype(BF16)
        bias = by_block([rows[0:1] for rows in bias_rows(pattern_ref, window)])

        def products(head):
            low = head * head_dim
            high = low + head_dim
            keys = qkv_ref[span, width + low : width + high]
            values = qkv_ref[span, 2 * width + low : 2 * width + high]
            scores = dot(keys, qk_t_ref[window, low:high, :])
            return scores, dot(values, d_mixed_t_ref[low:high, :])

        ready = products(0)
        for head in range(HEADS):
            low = head * head_dim
            high = low + head_dim
            scores, d_probs = ready
            if head + 1 < HEADS:
                ready = products(head + 1)
            keys_t = qk_t_ref[window, width + low : width + high, :]
            shift = bias - lse_ref[window, head : head + 1, :].reshape(1, 1, WINDOW)
            scores = scores.reshape(BLK, SLOT, WINDOW)
            probs = jnp.exp2(scores * factor + shift).reshape(WINDOW, WINDOW)
            d_values_t = dot_nt(d_mixed_t_ref[low:high, :], probs.astype(BF16))
            inner = jnp.sum(d_probs * probs, axis=0, keepdims=True)
            d_scores = (probs * (d_probs - inner) * scale).astype(BF16)
            d_keys_t = dot_nt(qk_t_ref[window, low:high, :], d_scores)
            d_qkv_t_ref[low:high, :] = dot(keys_t, d_scores).astype(BF16)
            d_qkv_t_ref[width + low : width + high, :] = d_keys_t.astype(BF16)
            d_qkv_t_ref[2 * width + low : 2 * width + high, :] = d_values_t.astype(BF16)
        d_qkv = jnp.transpose(d_qkv_t_ref[...])
        d_qkv_ref[span, :] = d_qkv
        _, normalized, _ = norm_stats(hilbert_ref[span, :])
        normed = (normalized * gain_ref[...]).astype(BF16)
        g_qkv_t_ref[...] += dot(d_qkv_t_ref[...], normed)
        d_normed = dot_nt(d_qkv, w_qkv_ref[...])
        g_gain_ref[0:1, :] += jnp.sum(d_normed * normalized, axis=0, keepdims=True)

    core, x, y = places()
    spread = AROUND_Y * PIECE
    for half, target in enumerate((own_ref, other_ref)):
        for start in range(AROUND_X):
            target[start, spread : spread + 8, :] = g_gain_ref[...]
        for number in range(AROUND_X * AROUND_Y):
            for side in range(CORES):
                row = (side * AROUND_X * AROUND_Y + number) * PIECE
                block, inside = row // width, row % width
                to_x = (number // AROUND_Y) ^ x
                to_y = pl.multiple_of(((number % AROUND_Y) ^ y) * PIECE, PIECE)

                @pl.when(core == side ^ half)
                def _(target=target, row=row, block=block, inside=inside, to_x=to_x, to_y=to_y):
                    if block < 3:
                        piece = g_qkv_t_ref[row : row + PIECE, :]
                    else:
                        piece = g_out_ref[inside : inside + PIECE, :]
                    target[to_x, pl.ds(to_y, PIECE), :] = piece


def places():
    here = lax.axis_index("seq")
    return lax.axis_index("batch"), lax.rem(here, AROUND_X), lax.div(here, AROUND_X * AROUND_Z)


def input_grad_kernel(
    route_ref,
    landing_ref,
    order_ref,
    gain_ref,
    w_qkv_ref,
    hilbert_ref,
    d_qkv_ref,
    upstream_ref,
    out_ref,
    local_ref,
    r0,
    r1,
    r2,
    r3,
    spread_ref,
    moved_ref,
    both_ref,
):
    total, width = hilbert_ref.shape

    @pl.loop(0, total // WINDOW)
    def _(window):
        span = pl.ds(pl.multiple_of(window * WINDOW, WINDOW), WINDOW)
        _, normalized, inverse_std = norm_stats(hilbert_ref[span, :])
        d_hat = dot_nt(d_qkv_ref[span, :], w_qkv_ref[...]) * gain_ref[...]
        branch = inverse_std * (
            d_hat
            - jnp.mean(d_hat, axis=-1, keepdims=True)
            - normalized * jnp.mean(d_hat * normalized, axis=-1, keepdims=True)
        )
        both_ref[span, 0:width] = out_ref[span, :]
        both_ref[span, width:] = (upstream_ref[span, :].astype(F32) + branch).astype(BF16)

    scatter_rows(order_ref, both_ref, spread_ref, moved_ref)
    leave(route_ref, landing_ref, moved_ref, local_ref, (r0, r1, r2, r3))


def scale_kernel(factor, gain_sum_ref, own_ref, other_ref, gain_ref, qkv_ref, out_ref, turn_ref):
    width = out_ref.shape[1]
    core, x, y = places()
    for half, source in enumerate((own_ref, other_ref)):
        for number in range(AROUND_X * AROUND_Y):
            from_x = (number // AROUND_Y) ^ x
            from_y = (number % AROUND_Y) ^ y
            start = pl.multiple_of((from_x * AROUND_Y + from_y) * PIECE, PIECE)
            piece = source[pl.ds(start, PIECE), :] * factor
            for side in range(CORES):
                row = (side * AROUND_X * AROUND_Y + number) * PIECE
                block, inside = row // width, row % width

                @pl.when(core == side ^ half)
                def _(piece=piece, row=row, block=block, inside=inside):
                    if block < 3:
                        turn_ref[row : row + PIECE, :] = piece
                    else:
                        out_ref[inside : inside + PIECE, :] = piece
    qkv_ref[...] = jnp.transpose(turn_ref[...])
    gain_ref[...] = gain_sum_ref[0:1, :] * factor


VMEM = pl.BlockSpec(memory_space=pltpu.VMEM)
SMEM = pl.BlockSpec(memory_space=pltpu.SMEM)
HBM = pl.BlockSpec(memory_space=pltpu.HBM)


def params(mebibytes):
    return pltpu.CompilerParams(vmem_limit_bytes=mebibytes << 20)


def in_hbm(*arrays):
    return [pltpu.with_memory_space_constraint(array, pltpu.HBM) for array in arrays]


def shape_of(*dims, dtype=BF16):
    return jax.ShapeDtypeStruct(dims, dtype)


def whole(array):
    return pl.BlockSpec(array.shape, lambda i: (0,) * array.ndim)


def pack(route, rows, labelled):
    width = rows.shape[1]
    tall = MOST * SLOT + (LABEL_ROWS if labelled else 0)
    return pl.pallas_call(
        pack_kernel,
        out_shape=[shape_of(tall, width)] * CHANNELS,
        in_specs=[HBM, HBM],
        out_specs=[VMEM] * CHANNELS,
        scratch_shapes=[
            pltpu.SMEM(route.shape, jnp.int32),
            pltpu.VMEM(rows.shape, BF16),
            pltpu.SemaphoreType.DMA((2,)),
        ],
        compiler_params=params(8),
        cost_estimate=pl.CostEstimate(flops=0, bytes_accessed=1 << 20, transcendentals=0),
        name="pack_slots",
    )(*in_hbm(route, rows))


def restore(route, local, arrivals):
    total, width = local.shape
    return pl.pallas_call(
        restore_kernel,
        out_shape=[shape_of(total, width // 2)] * 2,
        in_specs=[SMEM] + [VMEM] * (1 + CHANNELS),
        out_specs=[VMEM] * 2,
        compiler_params=params(8),
        cost_estimate=pl.CostEstimate(flops=0, bytes_accessed=3 << 20, transcendentals=0),
        name="restore_slots",
    )(route, local, *arrivals)


def forward(route, pattern, order, points, arrivals, gain, w_qkv, w_out):
    total, width = points.shape
    windows = total // WINDOW
    outs = pl.pallas_call(
        forward_kernel,
        out_shape=[
            shape_of(total, width),
            shape_of(total, width),
            shape_of(total, 3 * width),
            shape_of(windows, 2 * width, WINDOW),
            shape_of(windows, width, WINDOW),
            shape_of(windows, HEADS, WINDOW, dtype=F32),
            shape_of(CHANNELS * MOST, dtype=jnp.int32),
        ],
        in_specs=[HBM] * 7 + [VMEM] * CHANNELS,
        out_specs=[VMEM] * 6 + [SMEM],
        scratch_shapes=[
            pltpu.SMEM(route.shape, jnp.int32),
            pltpu.SMEM(pattern.shape, jnp.int32),
            pltpu.VMEM(order.shape, jnp.int32),
            pltpu.VMEM(gain.shape, F32),
            pltpu.VMEM(w_qkv.shape, BF16),
            pltpu.VMEM(w_out.shape, BF16),
            pltpu.SemaphoreType.DMA((7,)),
            pltpu.VMEM((total, width), BF16),
            pltpu.VMEM((total, SLOT), jnp.int32),
            pltpu.VMEM((WINDOW, total), BF16),
            pltpu.VMEM((total, width), BF16),
            pltpu.VMEM((width, WINDOW), BF16),
            pltpu.VMEM((3 * width, width), BF16),
            pltpu.VMEM((3, WINDOW, WINDOW), F32),
            pltpu.VMEM((2, WINDOW, WINDOW), BF16),
        ],
        compiler_params=params(32),
        cost_estimate=pl.CostEstimate(
            flops=12 << 30, bytes_accessed=8 << 20, transcendentals=4 << 20
        ),
        name="window_forward",
    )(*in_hbm(route, pattern, order, points, gain, w_qkv, w_out), *arrivals)
    return outs[0], outs[1:6], outs[6]


def backward(route, landing, pattern, order, grads, arrivals, gain, w_qkv, w_out, saved):
    total, width = grads.shape
    tall = AROUND_Y * PIECE + 8
    outs_shape = [
        shape_of(total, 3 * width),
        shape_of(total, width),
        shape_of(AROUND_X, tall, width, dtype=F32),
        shape_of(AROUND_X, tall, width, dtype=F32),
    ]
    return pl.pallas_call(
        backward_kernel,
        grid=(1,),
        out_shape=outs_shape,
        in_specs=[SMEM, SMEM, SMEM]
        + [whole(array) for array in (order, grads, *arrivals)]
        + [whole(array) for array in (gain, w_qkv, w_out, *saved)],
        out_specs=[whole(array) for array in outs_shape],
        scratch_shapes=[
            pltpu.VMEM((total, SLOT), jnp.int32),
            pltpu.VMEM((WINDOW, total), BF16),
            pltpu.VMEM((total, width), BF16),
            pltpu.VMEM((3 * width, WINDOW), BF16),
            pltpu.VMEM((width, WINDOW), BF16),
            pltpu.VMEM((3 * width, width), F32),
            pltpu.VMEM((width, width), F32),
            pltpu.VMEM((8, width), F32),
        ],
        compiler_params=params(36),
        cost_estimate=pl.CostEstimate(
            flops=20 << 30, bytes_accessed=8 << 20, transcendentals=4 << 20
        ),
        name="window_backward",
    )(route, landing, pattern, order, grads, *arrivals, gain, w_qkv, w_out, *saved)


def input_grad(route, landing, order, gain, w_qkv, hilbert, d_qkv, upstream, out):
    total, width = hilbert.shape
    outs_shape = [shape_of(total, 2 * width)] + [shape_of(MOST * SLOT, 2 * width)] * CHANNELS
    outs = pl.pallas_call(
        input_grad_kernel,
        grid=(1,),
        out_shape=outs_shape,
        in_specs=[SMEM, SMEM, whole(order)]
        + [whole(array) for array in (gain, w_qkv, hilbert, d_qkv, upstream, out)],
        out_specs=[whole(array) for array in outs_shape],
        scratch_shapes=[
            pltpu.VMEM((WINDOW, total), BF16),
            pltpu.VMEM((total, 2 * width), BF16),
            pltpu.VMEM((total, 2 * width), BF16),
        ],
        compiler_params=params(24),
        cost_estimate=pl.CostEstimate(
            flops=2 << 30, bytes_accessed=5 << 20, transcendentals=0
        ),
        name="input_grad",
    )(route, landing, order, gain, w_qkv, hilbert, d_qkv, upstream, out)
    return outs[0], outs[1:]


def scale_sums(gain_sum, own, other, factor):
    width = own.shape[1]
    return pl.pallas_call(
        functools.partial(scale_kernel, factor),
        out_shape=[
            shape_of(1, width, dtype=F32),
            shape_of(width, 3 * width, dtype=F32),
            shape_of(width, width, dtype=F32),
        ],
        in_specs=[VMEM] * 3,
        out_specs=[VMEM] * 3,
        scratch_shapes=[pltpu.VMEM((3 * width, width), F32)],
        compiler_params=params(8),
        cost_estimate=pl.CostEstimate(flops=0, bytes_accessed=2 << 20, transcendentals=0),
        name="scale_sums",
    )(gain_sum, own, other)


def exchange(arrays):
    peers = lax.axis_size("seq")
    out = []
    for channel, array in enumerate(arrays):
        pairs = [(i, partner_of(i, channel)) for i in range(peers)]
        pairs = [(i, j) for i, j in pairs if 0 <= j < peers]
        out.append(lax.ppermute(array, "seq", pairs))
    return out


def swap_seq(array, bits):
    peers = lax.axis_size("seq")
    return lax.ppermute(array, "seq", [(i, i ^ bits) for i in range(peers)])


def swap_core(array):
    return lax.ppermute(array, "batch", [(0, 1), (1, 0)])


def four_way(pieces, step):
    came = [swap_seq(pieces[j], j * step) for j in (1, 2, 3)]
    return (pieces[0] + came[0]) + (came[1] + came[2])


def gather_four(piece, step):
    return jnp.concatenate([piece] + [swap_seq(piece, j * step) for j in (1, 2, 3)], axis=0)


def tie(wanted, first):
    return lax.optimization_barrier((wanted, first))


def body(points, gain, w_qkv, w_out, route, order, pattern, grad_out):
    rows, grads = points[0], grad_out[0]
    total, width = rows.shape
    route = route[0]
    order_row = order[0]
    seen = pattern[0]
    gain_row = gain.reshape(1, width)
    point_in = exchange(pack(route, rows, True))
    grad_in = exchange(pack(route, grads, False))
    out, saved, landing = forward(route, seen, order_row, rows, point_in, gain_row, w_qkv, w_out)
    d_qkv, upstream, own, other = backward(
        route, landing, seen, order_row, grads, grad_in, gain_row, w_qkv, w_out, saved
    )
    step_z, step_y = AROUND_X, AROUND_X * AROUND_Z
    spread = AROUND_Y * PIECE
    part = own + swap_core(other)
    local, backs = input_grad(
        route, landing, order_row, gain_row, w_qkv, saved[0], d_qkv, upstream, out
    )
    part = four_way([part[j] for j in range(AROUND_X)], 1)
    part, (local, backs) = tie(part, (local, backs))
    back = exchange(backs)
    gain_rows = part[spread:]
    part = four_way(
        [
            jnp.concatenate([part[j * PIECE : (j + 1) * PIECE], gain_rows], axis=0)
            for j in range(AROUND_Y)
        ],
        step_y,
    )
    part = four_way([part] * 4, step_z)
    part = part + swap_seq(part, 4 * step_z)
    gain_sum = part[PIECE:]
    part = gather_four(part[:PIECE], step_y)
    part, back = tie(part, back)
    part = gather_four(part, 1)
    part, (result, grad_points) = tie(part, restore(route, local, back))
    own, other = part, swap_core(part)
    factor = (lax.axis_size("batch") * lax.axis_size("seq") * total) ** (-0.5)
    g_gain, g_qkv, g_out = scale_sums(gain_sum, own, other, factor)
    return (result[None], grad_points[None], g_gain.reshape(width), g_qkv, g_out)


def solution(mesh):
    return jax.shard_map(
        body,
        mesh=mesh,
        in_specs=(
            P("batch", "seq", None),
            P(),
            P(),
            P(),
            P("batch", "seq"),
            P("batch", "seq", None),
            P("batch", "seq", None, None),
            P("batch", "seq", None),
        ),
        out_specs=(P("batch", "seq", None), P("batch", "seq", None), P(), P(), P()),
        check_vma=False,
    )
```
